32 devices in a mesh: dom: 2 (over y), dp: 16 (over z, x, core).
Axes of the slice: x: 2, y: 2, z: 4, core: 2. Of those that a mesh axis runs over, the one named last changes fastest.
Arguments:
- positions: float32 [1024, 128], P(('dom', 'dp')), may hold values from -6 to 6
- length_scale: float32 [1], replicated, may hold values from 16 to 128
- features: float32 [32768, 128], P('dp'), may hold values from -0.5 to 0.5
- labels: int32 [32768], P('dp'), may hold values 0 or 1
- batch_index: int32 [8192], P('dp'), may hold values from 0 to 2047
Outputs:
- moved: float32 [1024, 128], P(('dom', 'dp'))
- score: float32 [1024, 128], P(('dom', 'dp'))
The draws below stay inside these ranges and needn't reach their ends.
Inputs may be any that keep to these rules, and one draw needn't show every extreme that they name: `batch_index`: an index into the 2048 feature rows of the same dp index.
All inputs are finite; a program needn't handle non-finite values. No bound on the sum of `labels` on one device may be relied on, other than what follows from the above.
Results may differ from the reference program's by a relative error of at most 0.0001.
Values sent between devices are 32-bit elements; how exact they have to be, the bound alone decides.
No kernel may reach another device: no remote copies, remote signals or barrier semaphores. Data moves between devices by JAX's collectives and lax.ppermute only.
A program may use at most 64 MiB of HBM per device.

```python
import math
import jax
import jax.numpy as jnp
from jax import lax

D = 128
P_DEV = 32
ROWS_DEV = 512
STEPS = 2
POOL_DEV = 2048
PARTICLES = 1024
ROWS_ALL = 8192
POOL_ALL = 32768
N_DP = 16


def draw_positions(key, part):
    centre_key = jax.random.fold_in(key, 11)
    member_key = jax.random.fold_in(key, 12)
    jitter_key = jax.random.fold_in(key, 13)
    member = jax.random.randint(member_key, (PARTICLES,), 0, 8)
    one_hot = (member[:, None] == jnp.arange(8, dtype=jnp.int32)[None, :]).astype(jnp.float32)
    centres = jax.random.normal(centre_key, (8, D), jnp.float32)
    jitter = 0.35 * jax.random.normal(jitter_key, (PARTICLES, D), jnp.float32)
    drawn = jnp.dot(one_hot, centres, precision=lax.Precision.HIGHEST) + jitter
    return jnp.clip(drawn, -6.0, 6.0)


def set_ends(entries, rng, smallest, high):
    place = [jax.random.randint(jax.random.fold_in(rng, axis), (), 0, length) for axis, length in enumerate(entries.shape)]
    widest = entries.shape.index(max(entries.shape))
    next_to = place[:widest] + [(place[widest] + 1) % entries.shape[widest]] + place[widest + 1:]
    return entries.at[tuple(place)].set(smallest).at[tuple(next_to)].set(high)


def steps_of(rng, dims, split, smallest, top_value):
    def one(dim, parts):
        draws = jax.random.uniform(jax.random.fold_in(jax.random.fold_in(rng, 6), dim), (parts,), jnp.float32, smallest / len(split), top_value / len(split))
        return jnp.repeat(jnp.exp(draws), dims[dim] // parts).reshape((-1,) + (1,) * (len(dims) - dim - 1))

    gain = one(*split[0])
    for cut in split[1:]:
        gain = gain * one(*cut)
    return gain


def bell_draw(rng, shape, scale, bound, cuts=(), kind=jnp.bfloat16):
    result = jax.random.normal(rng, shape, jnp.float32) * scale
    if len(cuts) > 0:
        result = steps_of(rng, shape, cuts, -0.22, 0.18) * result
    return jnp.clip(result, min=-bound, max=bound).astype(kind)


def setup_inputs(seed: int = 0) -> dict:
    key_of = jax.random.split(jax.random.key(seed), 6)
    positions = draw_positions(jax.random.fold_in(key_of[5], 71), 0)
    length_scale = jnp.clip(jnp.exp(jax.random.uniform(key_of[1], (1,), jnp.float32, math.log(16.0), math.log(128.0))), 16.0, 128.0)
    features = bell_draw(key_of[2], (POOL_ALL, D), D ** -0.5, 0.5, ((0, 16),), jnp.float32)
    labels = set_ends((jax.random.randint(key_of[3], (POOL_ALL,), 0, 2) < 1).astype(jnp.int32), jax.random.fold_in(key_of[3], 1), 0, 1)
    batch_index = set_ends(jax.random.randint(key_of[4], (ROWS_ALL,), 0, POOL_DEV), jax.random.fold_in(key_of[4], 1), 0, POOL_DEV - 1).astype(jnp.int32)
    return {"positions": positions, "length_scale": length_scale, "features": features, "labels": labels, "batch_index": batch_index}


HIGH = lax.Precision.HIGHEST
STEP_SIZE = 2.0

def likelihood(block, rows, targets, scale):
    logits = jnp.dot(block, rows.T, precision=HIGH, preferred_element_type=jnp.float32)
    resid = targets[None, :] - jax.nn.sigmoid(logits)
    return jnp.dot(resid, rows, precision=HIGH, preferred_element_type=jnp.float32) * scale

def displace(aimed, sources, source_score, spread):
    square_a = lax.optimization_barrier(jnp.sum(aimed * aimed, axis=1))
    square_b = lax.optimization_barrier(jnp.sum(sources * sources, axis=1))
    inner = jnp.dot(aimed, sources.T, precision=HIGH, preferred_element_type=jnp.float32)
    dist = square_a[:, None] + square_b[None, :] - 2.0 * inner
    kernel = lax.rsqrt(1.0 + dist / spread)
    cubed = kernel * kernel * kernel
    drive = jnp.dot(kernel, source_score, precision=HIGH, preferred_element_type=jnp.float32)
    pulled = jnp.dot(cubed, sources, precision=HIGH, preferred_element_type=jnp.float32)
    return drive + (aimed * lax.optimization_barrier(jnp.sum(cubed, axis=1))[:, None] - pulled) / spread

def reference(positions, length_scale, features, labels, batch_index):
    owner = jnp.arange(ROWS_DEV * N_DP, dtype=jnp.int32) // ROWS_DEV * POOL_DEV
    picked = (batch_index + owner).astype(jnp.int32)
    rows = features[picked]
    targets = labels[picked].astype(jnp.float32)
    scale = 1.0 / math.sqrt(ROWS_DEV * N_DP)
    spread = length_scale[0]
    current = positions
    blocks = PARTICLES // P_DEV
    score = current
    for iteration in range(STEPS):
        shaped = current.reshape(blocks, P_DEV, D)
        gradient = lax.map(lambda block: likelihood(block, rows, targets, scale), shaped)
        score = gradient.reshape(PARTICLES, D) - current
        moves = lax.map(lambda block: displace(block, current, score, spread), shaped)
        current = current + STEP_SIZE / PARTICLES * moves.reshape(PARTICLES, D)
    return (current, score)
```

```python
import math

import jax
import jax.numpy as jnp
from jax import lax
from jax.sharding import Mesh, PartitionSpec as P

STEPS = 2
STEP_SIZE = 2.0
HIGH = lax.Precision.HIGHEST


def dot(a, b):
    return jnp.dot(a, b, precision=HIGH, preferred_element_type=jnp.float32)


def dot_t(a, b):
    return lax.dot_general(a, b, (((1,), (1,)), ((), ())), precision=HIGH, preferred_element_type=jnp.float32)


def likelihood(block, rows, targets, scale):
    resid = targets[None, :] - jax.nn.sigmoid(dot_t(block, rows))
    return dot(resid, rows) * scale


def inverse_root(aimed, sources, spread):
    square_a = jnp.sum(aimed * aimed, axis=1)
    square_b = jnp.sum(sources * sources, axis=1)
    dist = square_a[:, None] + square_b[None, :] - 2.0 * dot_t(aimed, sources)
    return lax.rsqrt(1.0 + dist / spread)


def partial_move(aimed, sources, grads, own, spread):
    drive = dot(inverse_root(aimed, sources, spread), grads)
    kernel = inverse_root(aimed, own, spread)
    cubed = kernel * kernel * kernel
    pulled = dot(cubed, own)
    return drive - dot(kernel, own) + (aimed * jnp.sum(cubed, axis=1)[:, None] - pulled) / spread


def shifted(x, axis, offset):
    size = lax.axis_size(axis)
    return lax.ppermute(x, axis, [(i, (i + offset) % size) for i in range(size)])


def spread_over(x, axes):
    size = lax.axis_size(axes)
    tiled = jnp.broadcast_to(x[None], (size,) + x.shape)
    return lax.all_to_all(tiled, axes, 0, 0, tiled=True)


def summed_over(x, axes):
    return jnp.sum(lax.all_to_all(x, axes, 0, 0, tiled=True), axis=0)


def shards(positions, length_scale, features, labels, batch_index):
    doms, chips, cores = lax.axis_size("dom"), lax.axis_size("chip"), lax.axis_size("core")
    local, width = positions.shape
    total = local * doms * chips * cores
    scale = 1.0 / math.sqrt(batch_index.shape[0] * chips * cores)
    factor = STEP_SIZE / total
    spread = length_scale[0]
    dom, chip = lax.axis_index("dom"), lax.axis_index("chip")

    def all_cores(x):
        return [x] + [shifted(x, "core", o) for o in range(1, cores)]

    def all_doms(x):
        return [x] + [shifted(x, "dom", o) for o in range(1, doms)]

    rows = jnp.concatenate(all_cores(features[batch_index]), 0)
    targets = jnp.concatenate(all_cores(labels[batch_index].astype(jnp.float32)), 0)

    def flat(blocks):
        return jnp.concatenate([b.reshape(-1, width) for b in blocks], 0)

    def own_of(blocks):
        return flat([lax.dynamic_index_in_dim(b, chip, 0) for b in blocks])

    current = positions
    for iteration in range(STEPS):
        last = iteration == STEPS - 1
        near = spread_over(current, "chip")
        by_dom = all_doms(near)
        if last:
            aimed = near
            graded = by_dom
        else:
            aimed = jnp.roll(jnp.stack(by_dom[:1] + by_dom[:0:-1]), dom, axis=0)
            graded = [near]
        grads = [likelihood(b.reshape(-1, width), rows, targets, scale) for b in graded]
        sources = [s for b in graded for s in all_cores(b)]
        source_grads = [s for g in grads for s in all_cores(g)]
        moves = partial_move(aimed.reshape(-1, width), flat(sources), flat(source_grads), own_of(sources), spread)
        if last:
            both = jnp.concatenate([moves.reshape(chips, local, width), grads[0].reshape(chips, local, width)], 1)
            result = summed_over(both, "chip")
            score = result[local:] - current
            current = current + factor * result[:local]
        else:
            moves = summed_over(moves.reshape(doms * chips, local, width), ("dom", "chip"))
            current = current + factor * moves
    return (current, score)


def solution(mesh):
    doms, dp = mesh.shape["dom"], mesh.shape["dp"]
    cores = 2 if dp % 2 == 0 else 1
    inner = Mesh(mesh.devices.reshape(doms, dp // cores, cores), ("dom", "chip", "core"))
    dp_axes = ("chip", "core")
    placed = (P(("dom",) + dp_axes, None), P(), P(dp_axes, None), P(dp_axes), P(dp_axes))
    return jax.shard_map(
        shards,
        mesh=inner,
        in_specs=placed,
        out_specs=(P(("dom",) + dp_axes, None), P(("dom",) + dp_axes, None)),
        check_vma=False,
    )
```

```python
import functools
import math

import jax
import jax.numpy as jnp
from jax import lax
from jax.experimental import pallas as pl
from jax.experimental.pallas import tpu as pltpu
from jax.sharding import Mesh, PartitionSpec as P

STEPS = 2
STEP_SIZE = 2.0
F32, BF16 = jnp.float32, jnp.bfloat16
ROW_CHUNK = 256
SOURCE_CHUNK = 256
VMEM_LIMIT = 48 << 20


def parts(x, count):
    out = []
    for _ in range(count - 1):
        piece = x.astype(BF16)
        out.append(piece)
        x = x - piece.astype(F32)
    out.append(x.astype(BF16))
    return out


def dot(a, b):
    return jnp.dot(a, b, preferred_element_type=F32)


def dot_t(a, b):
    return lax.dot_general(a, b, (((1,), (1,)), ((), ())), preferred_element_type=F32)


def lanes(*pieces):
    return jnp.concatenate(pieces, axis=1)


def folded(x):
    half = x.shape[1] // 2
    return x[:, :half] + x[:, half:]


def grad_kernel(scale, place_ref, x_ref, rows_a_ref, rows_b_ref, targets_a_ref, targets_b_ref, out_ref):
    count = out_ref.shape[0]
    if count == x_ref.shape[0]:
        x = x_ref[...]
    else:
        x = x_ref[pl.ds(pl.multiple_of(place_ref[0] * count, count), count), :]
    high, low = parts(x, 2)
    wide = lanes(high, low, high, low)
    total = None
    for rows_ref, targets_ref in ((rows_a_ref, targets_a_ref), (rows_b_ref, targets_b_ref)):
        for start in range(0, rows_ref.shape[0], ROW_CHUNK):
            span = slice(start, start + ROW_CHUNK)
            row_high, row_low = parts(rows_ref[span, :], 2)
            logits = dot_t(wide, lanes(row_high, row_high, row_low, row_low))
            resid = targets_ref[:, span] - 1.0 / (1.0 + jnp.exp(-logits))
            resid_high, resid_low = parts(resid, 2)
            both = lanes(row_high, row_low)
            added = dot(resid_high, both) + dot(resid_low, both)
            total = added if total is None else total + added
    out_ref[...] = folded(total) * scale


def move_kernel(last, local, place_ref, spread_ref, mine_ref, pair_ref, grad_ref, pair_grad_ref, out_ref, acc_ref, kern_ref):
    dom, chip = place_ref[0], place_ref[1]
    inverse = 1.0 / spread_ref[0]
    width = mine_ref.shape[1]
    block = acc_ref.shape[0] if last else grad_ref.shape[0]
    own_span = pl.ds(pl.multiple_of(dom * block, block), block)
    aimed = mine_ref[own_span, :] if last else mine_ref[...]
    count = aimed.shape[0]
    doms = count // block
    high, mid, low = parts(aimed, 3)
    wide = lanes(high, mid, high, mid, high, low)
    square_a = jnp.sum(aimed * aimed, axis=1, keepdims=True)
    starts = [pl.multiple_of(d * block + chip * local, local) for d in range(doms)]
    if last:
        own_aimed = [mine_ref[pl.ds(pl.multiple_of(dom * block + chip * local, local), local), :]]
    else:
        own_aimed = [mine_ref[pl.ds(s, local), :] for s in starts]
    own_cubed = [jnp.zeros((local, 1), F32) for _ in starts]
    own_pulled = [jnp.zeros((local, 2 * width), F32) for _ in starts]
    ones = jnp.ones((8, 3 * width), BF16)
    first = True
    for source_ref, source_grad_ref in ((mine_ref, grad_ref), (pair_ref, pair_grad_ref)):
        for start in range(0, source_grad_ref.shape[0], SOURCE_CHUNK):
            if last:
                source = source_ref[start:start + SOURCE_CHUNK, :]
            else:
                source = source_ref[pl.ds(pl.multiple_of(dom * block + start, SOURCE_CHUNK), SOURCE_CHUNK), :]
            s_high, s_mid, s_low = parts(source, 3)
            inner = dot_t(wide, lanes(s_high, s_high, s_mid, s_mid, s_low, s_high))
            square_b = dot_t(ones, lanes(*parts(source * source, 3)))[:1, :]
            kernel = lax.rsqrt(1.0 + (square_a + square_b - 2.0 * inner) * inverse)
            kern_ref[...] = kernel
            k_high, k_low = parts(kernel, 2)
            grads = lanes(*parts(source_grad_ref[start:start + SOURCE_CHUNK, :], 2))
            drive = dot(k_high, grads) + dot(k_low, grads)
            if first:
                acc_ref[...] = drive
            else:
                acc_ref[...] += drive
            first = False
            pulls = lanes(*parts(source, 2))
            for i, s in enumerate(starts):
                own = kern_ref[pl.ds(s, local), :]
                cubed = own * own * own
                own_cubed[i] = own_cubed[i] + jnp.sum(cubed, axis=1, keepdims=True)
                w_high, w_low = parts(own + cubed * inverse, 2)
                own_pulled[i] = own_pulled[i] + dot(w_high, pulls) + dot(w_low, pulls)
    for i, s in enumerate(starts):
        extra = own_aimed[i] * (own_cubed[i] * inverse) - folded(own_pulled[i])
        acc_ref[pl.ds(s, local), :] += lanes(extra, jnp.zeros_like(extra))
    if last:
        moves = folded(acc_ref[...])
        for j in range(block // local):
            out_ref[j, :local, :] = moves[j * local:(j + 1) * local, :]
            out_ref[j, local:, :] = grad_ref[pl.ds(pl.multiple_of(dom * block + j * local, local), local), :]
    else:
        out_ref[...] = folded(acc_ref[...])


SMEM_SPEC = pl.BlockSpec(memory_space=pltpu.SMEM)
VMEM_SPEC = pl.BlockSpec(memory_space=pltpu.VMEM)
PARAMS = pltpu.CompilerParams(vmem_limit_bytes=VMEM_LIMIT)


def likelihood(place, x, count, row_sets, scale):
    (rows_a, targets_a), (rows_b, targets_b) = row_sets
    width = x.shape[1]
    data = rows_a.shape[0] + rows_b.shape[0]
    return pl.pallas_call(
        functools.partial(grad_kernel, scale),
        out_shape=jax.ShapeDtypeStruct((count, width), F32),
        in_specs=[SMEM_SPEC] + [VMEM_SPEC] * 5,
        out_specs=VMEM_SPEC,
        compiler_params=PARAMS,
        cost_estimate=pl.CostEstimate(flops=16 * count * data * width, bytes_accessed=0, transcendentals=count * data),
        name="grad",
    )(place, x, rows_a, rows_b, targets_a, targets_b)


def partial_move(place, spread, mine, pair, grads, pair_grads, block, local, last):
    width = mine.shape[1]
    count = block if last else mine.shape[0]
    shape = (block // local, 2 * local, width) if last else (count, width)
    return pl.pallas_call(
        functools.partial(move_kernel, last, local),
        out_shape=jax.ShapeDtypeStruct(shape, F32),
        in_specs=[SMEM_SPEC] * 2 + [VMEM_SPEC] * 4,
        out_specs=VMEM_SPEC,
        scratch_shapes=[pltpu.VMEM((count, 2 * width), F32), pltpu.VMEM((count, SOURCE_CHUNK), F32)],
        compiler_params=PARAMS,
        cost_estimate=pl.CostEstimate(flops=40 * count * grads.shape[0] * width, bytes_accessed=0, transcendentals=0),
        name="move",
    )(place, spread, mine, pair, grads, pair_grads)


def swapped(x):
    return lax.ppermute(x, "core", [(0, 1), (1, 0)])


def shards(positions, length_scale, features, labels, batch_index):
    doms, chips, cores = lax.axis_size("dom"), lax.axis_size("chip"), lax.axis_size("core")
    local, width = positions.shape
    block = chips * local
    scale = 1.0 / math.sqrt(batch_index.shape[0] * chips * cores)
    factor = STEP_SIZE / (local * doms * chips * cores)
    place = jnp.stack([lax.axis_index("dom"), lax.axis_index("chip")]).astype(jnp.int32)
    everywhere = ("dom", "chip")

    def spread_out(x):
        tiled = jnp.broadcast_to(x[None], (doms * chips,) + x.shape)
        return lax.all_to_all(tiled, everywhere, 0, 0, tiled=True).reshape(-1, width)

    rows = features[batch_index]
    targets = labels[batch_index].astype(F32)[None, :]
    row_sets = ((rows, targets), (swapped(rows), swapped(targets)))

    current = positions
    for iteration in range(STEPS):
        last = iteration == STEPS - 1
        mine = spread_out(current)
        pair = swapped(mine)
        grads = likelihood(place, mine, mine.shape[0] if last else block, row_sets, scale)
        pair_grads = swapped(grads)
        moves = partial_move(place, length_scale, mine, pair, grads, pair_grads, block, local, last)
        if last:
            result = jnp.sum(lax.all_to_all(moves, "chip", 0, 0, tiled=True), axis=0)
            score = result[local:] - current
            current = current + factor * result[:local]
        else:
            moves = lax.all_to_all(moves.reshape(doms * chips, local, width), everywhere, 0, 0, tiled=True)
            current = current + factor * jnp.sum(moves, axis=0)
    return (current, score)


def solution(mesh):
    doms, dp = mesh.shape["dom"], mesh.shape["dp"]
    inner = Mesh(mesh.devices.reshape(doms, dp // 2, 2), ("dom", "chip", "core"))
    dp_axes = ("chip", "core")
    placed = (P(("dom",) + dp_axes, None), P(), P(dp_axes, None), P(dp_axes), P(dp_axes))
    return jax.shard_map(
        shards,
        mesh=inner,
        in_specs=placed,
        out_specs=(P(("dom",) + dp_axes, None), P(("dom",) + dp_axes, None)),
        check_vma=False,
    )
```

```python
import functools
import math

import jax
import jax.numpy as jnp
from jax import lax
from jax.experimental import pallas as pl
from jax.experimental.pallas import tpu as pltpu
from jax.sharding import Mesh, PartitionSpec as P

STEPS = 2
STEP_SIZE = 2.0
F32, BF16 = jnp.float32, jnp.bfloat16
ROW_CHUNK = 256
SOURCE_CHUNK = 256
VMEM_LIMIT = 32 << 20
LANES = 128


def parts(x, count):
    out = []
    for _ in range(count - 1):
        piece = x.astype(BF16)
        out.append(piece)
        x = x - piece.astype(F32)
    out.append(x.astype(BF16))
    return out


def dot(a, b):
    return jnp.dot(a, b, preferred_element_type=F32)


def dot_t(a, b):
    return lax.dot_general(a, b, (((1,), (1,)), ((), ())), preferred_element_type=F32)


def lanes(*pieces):
    return jnp.concatenate(pieces, axis=1)


def folded(x):
    half = x.shape[1] // 2
    return x[:, :half] + x[:, half:]


def chunks(refs, size):
    for ref in refs:
        for start in range(0, ref.shape[0], size):
            yield ref[start:start + size, :]


def tile_kernel(x_ref, out_ref):
    out_ref[...] = jnp.broadcast_to(x_ref[...][None], out_ref.shape)


def grad_kernel(scale, x_ref, rows_a_ref, rows_b_ref, targets_ref, out_ref):
    high, low = parts(-x_ref[...], 2)
    wide = lanes(high, low, high, low)
    total, start = None, 0
    for rows in chunks((rows_a_ref, rows_b_ref), ROW_CHUNK):
        row_high, row_low = parts(rows, 2)
        minus_logits = dot_t(wide, lanes(row_high, row_high, row_low, row_low))
        targets = targets_ref[:, start:start + rows.shape[0]]
        start += rows.shape[0]
        resid_high, resid_low = parts(targets - 1.0 / (1.0 + jnp.exp(minus_logits)), 2)
        both = lanes(row_high, row_low)
        added = dot(resid_high, both) + dot(resid_low, both)
        total = added if total is None else total + added
    out_ref[...] = folded(total) * scale


def kernel_of(aimed, inverse):
    high, mid, low = parts(aimed * (-2.0 * inverse), 3)
    wide = lanes(high, mid, high, mid, high, low)
    square_a = 1.0 + jnp.sum(aimed * aimed, axis=1, keepdims=True) * inverse
    ones = jnp.ones((8, 3 * aimed.shape[1]), BF16)

    def with_sources(source):
        s_high, s_mid, s_low = parts(source, 3)
        inner = dot_t(wide, lanes(s_high, s_high, s_mid, s_mid, s_low, s_high))
        square_b = dot_t(ones, lanes(*parts(source * source, 3)))[:1, :] * inverse
        return lax.rsqrt((square_a + square_b) + inner), lanes(s_high, s_mid)

    return with_sources


def weights_kernel(spread_ref, aimed_ref, *refs):
    source_refs, (high_ref, low_ref) = refs[:-2], refs[-2:]
    with_sources = kernel_of(aimed_ref[...], 1.0 / spread_ref[...])
    start = 0
    for source in chunks(source_refs, SOURCE_CHUNK):
        span = slice(start, start + source.shape[0])
        high_ref[:, span], low_ref[:, span] = parts(with_sources(source)[0], 2)
        start += source.shape[0]


def drive_kernel(local, high_ref, low_ref, *refs):
    grad_refs, riders, out_ref = refs[:2], refs[2:-1], refs[-1]
    grads = jnp.concatenate([lanes(*parts(ref[...], 2)) for ref in grad_refs], axis=0)
    drive = folded(dot(high_ref[...], grads) + dot(low_ref[...], grads))
    if not riders:
        out_ref[...] = drive
        return
    for j in range(out_ref.shape[0]):
        out_ref[j, :local, :] = drive[j * local:(j + 1) * local, :]
        out_ref[j, local:, :] = riders[0][j * local:(j + 1) * local, :]


def own_kernel(spread_ref, own_ref, *refs):
    source_refs, out_ref = refs[:-1], refs[-1]
    inverse = 1.0 / spread_ref[...]
    own = own_ref[...]
    with_sources = kernel_of(own, inverse)
    cubes, pulled = None, None
    for source in chunks(source_refs, SOURCE_CHUNK):
        kernel, pulls = with_sources(source)
        cubed = kernel * kernel * kernel
        high, low = parts(kernel + cubed * inverse, 2)
        cube, pull = jnp.sum(cubed, axis=1, keepdims=True), dot(high, pulls) + dot(low, pulls)
        cubes, pulled = (cube, pull) if cubes is None else (cubes + cube, pulled + pull)
    out_ref[...] = own * (cubes * inverse) - folded(pulled)


VMEM_SPEC = pl.BlockSpec(memory_space=pltpu.VMEM)


def run(kernel, out_shape, *args, flops=0):
    moved = sum(math.prod(a.shape) for a in args) * 4
    return pl.pallas_call(
        kernel,
        out_shape=out_shape,
        in_specs=[VMEM_SPEC] * len(args),
        out_specs=jax.tree.map(lambda _: VMEM_SPEC, out_shape),
        compiler_params=pltpu.CompilerParams(vmem_limit_bytes=VMEM_LIMIT),
        cost_estimate=pl.CostEstimate(flops=flops, bytes_accessed=moved, transcendentals=0),
    )(*args)


def array(*shape, dtype=F32):
    return jax.ShapeDtypeStruct(shape, dtype)


def swapped(x):
    return lax.ppermute(x, "core", [(0, 1), (1, 0)])


def picked(table, index):
    grid = table.astype(BF16).reshape(-1, LANES)
    major = lax.broadcasted_iota(jnp.int32, (grid.shape[0], index.shape[0]), 0) == (index // LANES)[None, :]
    minor = lax.broadcasted_iota(jnp.int32, (LANES, index.shape[0]), 0) == (index % LANES)[None, :]
    found = lax.dot_general(grid, major.astype(BF16), (((0,), (0,)), ((), ())), preferred_element_type=F32)
    return jnp.sum(jnp.where(minor, found, 0.0), axis=0, keepdims=True)


def shards(positions, length_scale, features, labels, batch_index):
    doms, chips, cores = lax.axis_size("dom"), lax.axis_size("chip"), lax.axis_size("core")
    local, width = positions.shape
    block = chips * local
    scale = 1.0 / math.sqrt(batch_index.shape[0] * chips * cores)
    factor = STEP_SIZE / (local * doms * chips * cores)
    dom, chip = lax.axis_index("dom"), lax.axis_index("chip")
    everywhere = ("dom", "chip")
    spread = length_scale.reshape(1, 1)

    rows = features[batch_index]
    targets = picked(labels, batch_index)
    pair_targets = swapped(targets)
    targets = jnp.concatenate([targets, pair_targets], axis=1)
    row_sets = (rows, swapped(rows), targets)
    data = rows.shape[0] * cores

    current = positions
    for iteration in range(STEPS):
        last = iteration == STEPS - 1
        if iteration == 0:
            tiled = run(tile_kernel, array(doms * chips, local, width), current)
        else:
            tiled = jnp.broadcast_to(current[None], (doms * chips, local, width))
        mine = lax.all_to_all(tiled, everywhere, 0, 0, tiled=True).reshape(-1, width)
        own_block = lax.dynamic_slice_in_dim(mine, dom * block, block, 0)
        if iteration == 0:
            current = lax.dynamic_slice_in_dim(own_block, chip * local, local, 0)
        pair = swapped(mine)
        if last:
            aimed, graded, sources = own_block, mine, (mine, pair)
        else:
            pair_block = lax.dynamic_slice_in_dim(pair, dom * block, block, 0)
            aimed, graded, sources = mine, own_block, (own_block, pair_block)
        count, found = aimed.shape[0], sum(s.shape[0] for s in sources)
        grads = run(
            functools.partial(grad_kernel, scale), array(graded.shape[0], width), graded, *row_sets,
            flops=16 * graded.shape[0] * data * width,
        )
        pair_grads = swapped(grads)
        high, low = run(
            weights_kernel, (array(count, found, dtype=BF16),) * 2, spread, aimed, *sources,
            flops=12 * count * found * width,
        )
        drive = functools.partial(drive_kernel, local)
        flops = 8 * count * found * width
        if last:
            rider = lax.dynamic_slice_in_dim(grads, dom * block, block, 0)
            shape = array(chips, 2 * local, width)
            moves = run(drive, shape, high, low, grads, pair_grads, rider, flops=flops)
        else:
            moves = run(drive, array(count, width), high, low, grads, pair_grads, flops=flops)
        moves = lax.all_to_all(
            moves.reshape(-1, moves.shape[-2] if last else local, width),
            "chip" if last else everywhere, 0, 0, tiled=True,
        )
        extra = run(own_kernel, array(local, width), spread, current, mine, pair, flops=flops // chips)
        result = jnp.sum(moves, axis=0)
        if last:
            score = result[local:] - current
        current = current + factor * (result[:local] + extra)
    return (current, score)


def solution(mesh):
    doms, dp = mesh.shape["dom"], mesh.shape["dp"]
    inner = Mesh(mesh.devices.reshape(doms, dp // 2, 2), ("dom", "chip", "core"))
    dp_axes = ("chip", "core")
    placed = (P(("dom",) + dp_axes, None), P(), P(dp_axes, None), P(dp_axes), P(dp_axes))
    return jax.shard_map(
        shards,
        mesh=inner,
        in_specs=placed,
        out_specs=(P(("dom",) + dp_axes, None), P(("dom",) + dp_axes, None)),
        check_vma=False,
    )
```

```python
import functools
import math

import jax
import jax.numpy as jnp
from jax import lax
from jax.experimental import pallas as pl
from jax.experimental.pallas import tpu as pltpu
from jax.sharding import Mesh, PartitionSpec as P

STEPS = 2
STEP_SIZE = 2.0
F32, BF16 = jnp.float32, jnp.bfloat16
ROW_CHUNK = 256
SOURCE_CHUNK = 256
VMEM_LIMIT = 32 << 20
LANES = 128


def parts(x, count):
    out = []
    for _ in range(count - 1):
        piece = x.astype(BF16)
        out.append(piece)
        x = x - piece.astype(F32)
    out.append(x.astype(BF16))
    return out


def dot(a, b):
    return jnp.dot(a, b, preferred_element_type=F32)


def dot_t(a, b):
    return lax.dot_general(a, b, (((1,), (1,)), ((), ())), preferred_element_type=F32)


def lanes(*pieces):
    return jnp.concatenate(pieces, axis=1)


def folded(x):
    half = x.shape[1] // 2
    return x[:, :half] + x[:, half:]


def chunks(refs, size):
    for ref in refs:
        for start in range(0, ref.shape[0], size):
            yield ref[start:start + size, :]


def tile_kernel(x_ref, out_ref):
    out_ref[...] = jnp.broadcast_to(x_ref[...][None], out_ref.shape)


def grad_kernel(scale, x_ref, rows_a_ref, rows_b_ref, targets_ref, out_ref):
    high, low = parts(-x_ref[...], 2)
    wide = lanes(high, low, high, low)
    total, start = None, 0
    for rows in chunks((rows_a_ref, rows_b_ref), ROW_CHUNK):
        row_high, row_low = parts(rows, 2)
        minus_logits = dot_t(wide, lanes(row_high, row_high, row_low, row_low))
        targets = targets_ref[:, start:start + rows.shape[0]]
        start += rows.shape[0]
        resid_high, resid_low = parts(targets - 1.0 / (1.0 + jnp.exp(minus_logits)), 2)
        both = lanes(row_high, row_low)
        added = dot(resid_high, both) + dot(resid_low, both)
        total = added if total is None else total + added
    out_ref[...] = folded(total) * scale


def kernel_of(aimed, inverse):
    high, mid, low = parts(aimed * (-2.0 * inverse), 3)
    wide = lanes(high, mid, high, mid, high, low)
    square_a = 1.0 + jnp.sum(aimed * aimed, axis=1, keepdims=True) * inverse
    ones = jnp.ones((8, 3 * aimed.shape[1]), BF16)

    def with_sources(source):
        s_high, s_mid, s_low = parts(source, 3)
        inner = dot_t(wide, lanes(s_high, s_high, s_mid, s_mid, s_low, s_high))
        square_b = dot_t(ones, lanes(*parts(source * source, 3)))[:1, :] * inverse
        return lax.rsqrt((square_a + square_b) + inner), lanes(s_high, s_mid)

    return with_sources


def weights_kernel(inverse_ref, aimed_ref, own_ref, *refs):
    source_refs, (high_ref, low_ref, extra_ref) = refs[:-3], refs[-3:]
    inverse = inverse_ref[...]
    own, count = own_ref[...], aimed_ref.shape[0]
    with_sources = kernel_of(jnp.concatenate([aimed_ref[...], own], axis=0), inverse)
    start, cubes, pulled = 0, None, None
    for source in chunks(source_refs, SOURCE_CHUNK):
        span = slice(start, start + source.shape[0])
        start += source.shape[0]
        kernel, pulls = with_sources(source)
        high_ref[:, span], low_ref[:, span] = parts(kernel[:count], 2)
        mine = kernel[count:]
        cubed = mine * mine * mine
        pull = dot(jnp.concatenate(parts(mine + cubed * inverse, 2), axis=0), pulls)
        cube = jnp.sum(cubed, axis=1, keepdims=True)
        cubes, pulled = (cube, pull) if cubes is None else (cubes + cube, pulled + pull)
    pulled = folded(pulled)
    extra_ref[...] = own * (cubes * inverse) - (pulled[:own.shape[0]] + pulled[own.shape[0]:])


def drive_kernel(local, riding, high_ref, low_ref, *refs):
    grad_refs, riders, out_ref = refs[:2], refs[2:-1], refs[-1]
    grads = jnp.concatenate([lanes(*parts(ref[...], 2)) for ref in grad_refs], axis=0)
    drive = folded(dot(high_ref[...], grads) + dot(low_ref[...], grads))
    for j in range(out_ref.shape[0]):
        out_ref[j, :local, :] = drive[j * local:(j + 1) * local, :]
        if riding:
            out_ref[j, local:, :] = riders[0][j * local:(j + 1) * local, :]


VMEM_SPEC = pl.BlockSpec(memory_space=pltpu.VMEM)


def run(kernel, out_shape, *args, flops=0):
    moved = sum(math.prod(a.shape) for a in args) * 4
    return pl.pallas_call(
        kernel,
        out_shape=out_shape,
        in_specs=[VMEM_SPEC] * len(args),
        out_specs=jax.tree.map(lambda _: VMEM_SPEC, out_shape),
        compiler_params=pltpu.CompilerParams(vmem_limit_bytes=VMEM_LIMIT),
        cost_estimate=pl.CostEstimate(flops=flops, bytes_accessed=moved, transcendentals=0),
    )(*args)


def array(*shape, dtype=F32):
    return jax.ShapeDtypeStruct(shape, dtype)


def swapped(x):
    return lax.ppermute(x, "core", [(0, 1), (1, 0)])


def picked(table, index):
    grid = table.astype(BF16).reshape(-1, LANES)
    major = lax.broadcasted_iota(jnp.int32, (grid.shape[0], index.shape[0]), 0) == (index // LANES)[None, :]
    minor = lax.broadcasted_iota(jnp.int32, (LANES, index.shape[0]), 0) == (index % LANES)[None, :]
    found = lax.dot_general(grid, major.astype(BF16), (((0,), (0,)), ((), ())), preferred_element_type=F32)
    return jnp.sum(jnp.where(minor, found, 0.0), axis=0, keepdims=True)


def shards(positions, length_scale, features, labels, batch_index):
    doms, chips, cores = lax.axis_size("dom"), lax.axis_size("chip"), lax.axis_size("core")
    local, width = positions.shape
    block = chips * local
    scale = 1.0 / math.sqrt(batch_index.shape[0] * chips * cores)
    factor = STEP_SIZE / (local * doms * chips * cores)
    dom, chip = lax.axis_index("dom"), lax.axis_index("chip")
    everywhere = ("dom", "chip")

    rows = features[batch_index]
    targets = picked(labels, batch_index)
    pair_targets = swapped(targets)
    targets = jnp.concatenate([targets, pair_targets], axis=1)
    row_sets = (rows, swapped(rows), targets)
    inverse = (1.0 / length_scale).reshape(1, 1)
    data = rows.shape[0] * cores

    current = positions
    for iteration in range(STEPS):
        last = iteration == STEPS - 1
        if iteration == 0:
            tiled = run(tile_kernel, array(doms * chips, local, width), current)
        else:
            tiled = jnp.broadcast_to(current[None], (doms * chips, local, width))
        mine = lax.all_to_all(tiled, everywhere, 0, 0, tiled=True).reshape(-1, width)
        pair = swapped(mine)
        aimed = lax.dynamic_slice_in_dim(mine, dom * block, block, 0)
        if iteration == 0:
            current = lax.dynamic_slice_in_dim(mine, dom * block + chip * local, local, 0)
        found = mine.shape[0] * cores
        grads = run(
            functools.partial(grad_kernel, scale), array(*mine.shape), mine, *row_sets,
            flops=16 * mine.shape[0] * data * width,
        )
        pair_grads = swapped(grads)
        part = array(block, found, dtype=BF16)
        high, low, extra = run(
            weights_kernel, (part, part, array(local, width)), inverse, aimed, current, mine, pair,
            flops=12 * (block + local) * found * width,
        )
        riders = [lax.dynamic_slice_in_dim(grads, dom * block, block, 0)] if last else []
        moves = run(
            functools.partial(drive_kernel, local, last),
            array(chips, (2 if last else 1) * local, width), high, low, grads, pair_grads, *riders,
            flops=8 * block * found * width,
        )
        result = jnp.sum(lax.all_to_all(moves, "chip", 0, 0, tiled=True), axis=0)
        if last:
            score = result[local:] - current
        current = current + factor * (result[:local] + extra)
    return (current, score)


def solution(mesh):
    doms, dp = mesh.shape["dom"], mesh.shape["dp"]
    inner = Mesh(mesh.devices.reshape(doms, dp // 2, 2), ("dom", "chip", "core"))
    dp_axes = ("chip", "core")
    placed = (P(("dom",) + dp_axes, None), P(), P(dp_axes, None), P(dp_axes), P(dp_axes))
    return jax.shard_map(
        shards,
        mesh=inner,
        in_specs=placed,
        out_specs=(P(("dom",) + dp_axes, None), P(("dom",) + dp_axes, None)),
        check_vma=False,
    )
```
